32 devices in a mesh: groups: 2 (over y), tile: 4 (over z), col: 2 (over x), branch: 2 (over core).
Axes of the slice: x: 2, y: 2, z: 4, core: 2. Of those that a mesh axis runs over, the one named last changes fastest.
Arguments:
- alignment_tensor: float32 [4, 64, 256, 256], P(('groups', 'branch'), 'tile', 'col'), parts along dimension 0, may hold values from -6 to 6
- residue_grid: float32 [4, 256, 256, 128], P(('groups', 'branch'), 'tile', 'col'), parts along dimension 0, may hold values from -6 to 6
- mixing_scale_vector: float32 [256], replicated, may hold values from 0.1 to 1.9
- logit_offset_scale: float32 [128], replicated, may hold values from 0.1 to 1.9
- feedforward_scale: float32 [256], replicated, may hold values from 0.1 to 1.9
- product_scale_vector: float32 [256], replicated, may hold values from 0.1 to 1.9
- grid_scale_vector: float32 [128], replicated, may hold values from 0.1 to 1.9
- logit_offset_map: float32 [128, 8], replicated, may hold values from -0.5 to 0.5
- asking_mapping: bfloat16 [256, 256], replicated, may hold values from -0.375 to 0.375
- lookup_mapping: bfloat16 [256, 256], replicated, may hold values from -0.375 to 0.375
- content_mapping: bfloat16 [256, 256], replicated, may hold values from -0.375 to 0.375
- mixing_return_matrix: bfloat16 [256, 256], replicated, may hold values from -0.375 to 0.375
- alignment_widen_map: bfloat16 [256, 1024], replicated, may hold values from -0.375 to 0.375
- alignment_shrink_map: bfloat16 [1024, 256], replicated, may hold values from -0.1875 to 0.1875
- former_embedding_map: bfloat16 [256, 32], replicated, may hold values from -0.375 to 0.375
- latter_embedding_map: bfloat16 [256, 32], replicated, may hold values from -0.375 to 0.375
- product_return_map: float32 [1024, 128], replicated, may hold values from -1 to 1
- grid_widen_map: bfloat16 [128, 512], replicated, may hold values from -0.5 to 0.5
- grid_shrink_map: bfloat16 [512, 128], replicated, may hold values from -0.25 to 0.25
Outputs:
- alignment_revised: float32 [4, 64, 256, 256], P(('groups', 'branch'), 'tile', 'col'), parts along dimension 0
- grid_revised: float32 [4, 256, 256, 128], P(('groups', 'branch'), 'tile', 'col'), parts along dimension 0
The draws below stay inside these ranges and needn't reach their ends.
There are 2 independent parts, one for each index of `groups`. The reference program is written for one: setup_inputs(seed, part) draws one part's arguments, and reference() takes and returns one part's arrays. A program takes and returns all parts, laid end to end along the dimension named above; an argument that names none is the same for every part. Nothing has to cross between parts.
All inputs are finite; a program needn't handle non-finite values.
Results may differ from the reference program's by a relative error of at most 0.0075.
Values may be sent and summed in bfloat16 or wider, within the bound.
No kernel may reach another device: no remote copies, remote signals or barrier semaphores. Data moves between devices by JAX's collectives and lax.ppermute only.
A program may use at most 128 MiB of HBM per device.

```python
import jax
import jax.numpy as jnp
from jax import lax

ALIGN_FEATURES = 256
CZ = 128
HEADS = 8
TENSOR_FEATURES = 32
ALIGN_EXPANDED = 1024
PAIR_FF = 512
SEQUENCE_DEPTH = 64
CHAIN_LENGTH = 256
SAMPLE_TOTAL = 2


def levels(own_key, dims, split, low, top_value):
    def one(dim, parts):
        draws = jax.random.uniform(jax.random.fold_in(jax.random.fold_in(own_key, 6), dim), (parts,), jnp.float32, low / len(split), top_value / len(split))
        return jnp.repeat(jnp.exp(draws), dims[dim] // parts).reshape((-1,) + (1,) * (len(dims) - dim - 1))

    level = one(*split[0])
    for cut in split[1:]:
        level = level * one(*cut)
    return level


def gaussian(key, shape, scale, most, cuts=(), dtype=jnp.bfloat16):
    factor_of = levels(key, shape, cuts, -0.22, 0.18) if cuts else 1.0
    drawn = jax.random.normal(key, shape, jnp.float32) * scale * factor_of
    return jnp.minimum(jnp.maximum(drawn, -most), most).astype(dtype)


def setup_inputs(seed: int = 0, part: int = 0) -> dict:
    seeds = jax.random.split(jax.random.key(seed), 20)
    part_splits = jax.random.split(jax.random.fold_in(seeds[19], part), 20)
    alignment_tensor = gaussian(part_splits[0], (SAMPLE_TOTAL, SEQUENCE_DEPTH, CHAIN_LENGTH, ALIGN_FEATURES), 1.0, 6.0, ((0, 2), (1, 4), (2, 2)), jnp.float32)
    residue_grid = gaussian(part_splits[1], (SAMPLE_TOTAL, CHAIN_LENGTH, CHAIN_LENGTH, CZ), 1.0, 6.0, ((0, 2), (1, 4), (2, 2)), jnp.float32)
    mixing_scale_vector = jnp.clip(1.0 + 0.18 * jax.random.normal(seeds[2], (ALIGN_FEATURES,), jnp.float32), 0.1, 1.9)
    logit_offset_scale = jnp.clip(1.0 + 0.18 * jax.random.normal(seeds[3], (CZ,), jnp.float32), 0.1, 1.9)
    feedforward_scale = jnp.clip(1.0 + 0.18 * jax.random.normal(seeds[4], (ALIGN_FEATURES,), jnp.float32), 0.1, 1.9)
    product_scale_vector = jnp.clip(1.0 + 0.18 * jax.random.normal(seeds[5], (ALIGN_FEATURES,), jnp.float32), 0.1, 1.9)
    grid_scale_vector = jnp.clip(1.0 + 0.18 * jax.random.normal(seeds[6], (CZ,), jnp.float32), 0.1, 1.9)
    logit_offset_map = gaussian(seeds[7], (CZ, HEADS), CZ ** -0.5, 0.5, (), jnp.float32)
    asking_mapping = gaussian(seeds[8], (ALIGN_FEATURES, ALIGN_FEATURES), ALIGN_FEATURES ** -0.5, 0.375)
    lookup_mapping = gaussian(seeds[9], (ALIGN_FEATURES, ALIGN_FEATURES), ALIGN_FEATURES ** -0.5, 0.375)
    content_mapping = gaussian(seeds[10], (ALIGN_FEATURES, ALIGN_FEATURES), ALIGN_FEATURES ** -0.5, 0.375)
    mixing_return_matrix = gaussian(seeds[11], (ALIGN_FEATURES, ALIGN_FEATURES), ALIGN_FEATURES ** -0.5, 0.375)
    alignment_widen_map = gaussian(seeds[12], (ALIGN_FEATURES, ALIGN_EXPANDED), ALIGN_FEATURES ** -0.5, 0.375)
    alignment_shrink_map = gaussian(seeds[13], (ALIGN_EXPANDED, ALIGN_FEATURES), ALIGN_EXPANDED ** -0.5, 0.1875)
    former_embedding_map = gaussian(seeds[14], (ALIGN_FEATURES, TENSOR_FEATURES), ALIGN_FEATURES ** -0.5, 0.375)
    latter_embedding_map = gaussian(seeds[15], (ALIGN_FEATURES, TENSOR_FEATURES), ALIGN_FEATURES ** -0.5, 0.375)
    product_return_map = gaussian(seeds[16], (TENSOR_FEATURES * TENSOR_FEATURES, CZ), TENSOR_FEATURES ** -0.5, 1.0, (), jnp.float32)
    grid_widen_map = gaussian(seeds[17], (CZ, PAIR_FF), CZ ** -0.5, 0.5)
    grid_shrink_map = gaussian(seeds[18], (PAIR_FF, CZ), PAIR_FF ** -0.5, 0.25)
    return dict(alignment_tensor=alignment_tensor, residue_grid=residue_grid, mixing_scale_vector=mixing_scale_vector, logit_offset_scale=logit_offset_scale, feedforward_scale=feedforward_scale, product_scale_vector=product_scale_vector, grid_scale_vector=grid_scale_vector, logit_offset_map=logit_offset_map, asking_mapping=asking_mapping, lookup_mapping=lookup_mapping, content_mapping=content_mapping, mixing_return_matrix=mixing_return_matrix, alignment_widen_map=alignment_widen_map, alignment_shrink_map=alignment_shrink_map, former_embedding_map=former_embedding_map, latter_embedding_map=latter_embedding_map, product_return_map=product_return_map, grid_widen_map=grid_widen_map, grid_shrink_map=grid_shrink_map)


def standardize_features(x, gain):
    mean = lax.optimization_barrier(jnp.mean(x, axis=-1, keepdims=True))
    var = lax.optimization_barrier(jnp.mean((x - mean) ** 2, axis=-1, keepdims=True))
    return (x - mean) * lax.rsqrt(var + 1e-05) * gain

def lone_sample(alignment_tensor, residue_grid, mixing_scale_vector, logit_offset_scale, feedforward_scale, product_scale_vector, grid_scale_vector, logit_offset_map, asking_mapping, lookup_mapping, content_mapping, mixing_return_matrix, alignment_widen_map, alignment_shrink_map, former_embedding_map, latter_embedding_map, product_return_map, grid_widen_map, grid_shrink_map):
    subspace_total = logit_offset_map.shape[1]
    feature_extent = alignment_tensor.shape[-1]
    subspace_number = feature_extent // subspace_total
    bias = jnp.einsum('ijc,ch->hij', standardize_features(residue_grid, logit_offset_scale), logit_offset_map, precision=lax.Precision.HIGHEST)
    standardized_source = standardize_features(alignment_tensor, mixing_scale_vector).astype(jnp.bfloat16)
    asking_vectors = jnp.dot(standardized_source, asking_mapping, preferred_element_type=jnp.float32).astype(jnp.bfloat16)
    lookup_vectors = jnp.dot(standardized_source, lookup_mapping, preferred_element_type=jnp.float32).astype(jnp.bfloat16)
    content_vectors = jnp.dot(standardized_source, content_mapping, preferred_element_type=jnp.float32).astype(jnp.bfloat16)
    sample_portion = min(16, SEQUENCE_DEPTH)
    reformed = (SEQUENCE_DEPTH // sample_portion, sample_portion, CHAIN_LENGTH, subspace_total, subspace_number)

    def gated_softmax_mixing(items):
        qpart, kpart, vpart = items
        scores = jnp.einsum('sqhd,skhd->shqk', qpart.astype(jnp.float32), kpart.astype(jnp.float32)) / jnp.sqrt(jnp.float32(subspace_number)) + bias[None]
        weights = jax.nn.softmax(scores, axis=-1).astype(jnp.bfloat16)
        mixed = jnp.einsum('shqk,skhd->sqhd', weights.astype(jnp.float32), vpart.astype(jnp.float32))
        return mixed.astype(jnp.bfloat16).reshape(sample_portion, CHAIN_LENGTH, feature_extent)
    mixing_outcome = lax.map(gated_softmax_mixing, (asking_vectors.reshape(reformed), lookup_vectors.reshape(reformed), content_vectors.reshape(reformed))).reshape(SEQUENCE_DEPTH, CHAIN_LENGTH, feature_extent)
    alignment_activations = alignment_tensor + jnp.dot(mixing_outcome, mixing_return_matrix, preferred_element_type=jnp.float32)
    expanded_features = jax.nn.relu(jnp.dot(standardize_features(alignment_activations, feedforward_scale).astype(jnp.bfloat16), alignment_widen_map, preferred_element_type=jnp.float32)).astype(jnp.bfloat16)
    alignment_revised = alignment_activations + jnp.dot(expanded_features, alignment_shrink_map, preferred_element_type=jnp.float32)
    product_operands = standardize_features(alignment_tensor, product_scale_vector).astype(jnp.bfloat16)
    former_tensor = jnp.dot(product_operands, former_embedding_map, preferred_element_type=jnp.float32).astype(jnp.bfloat16)
    latter_tensor = jnp.dot(product_operands, latter_embedding_map, preferred_element_type=jnp.float32).astype(jnp.bfloat16)
    product_extent = former_tensor.shape[-1]
    latter_portion = min(16, CHAIN_LENGTH)
    former_portions = former_tensor.reshape(SEQUENCE_DEPTH, CHAIN_LENGTH // latter_portion, latter_portion, product_extent).transpose(1, 0, 2, 3)

    def outer_rows(fragment):
        tensor_product = jnp.einsum('era,eyq->ryaq', fragment.astype(jnp.float32), latter_tensor.astype(jnp.float32)) / SEQUENCE_DEPTH
        return jnp.dot(tensor_product.reshape(latter_portion, CHAIN_LENGTH, product_extent * product_extent), product_return_map, precision=lax.Precision.HIGHEST)
    update = lax.map(outer_rows, former_portions).reshape(CHAIN_LENGTH, CHAIN_LENGTH, -1)
    pair_mid = residue_grid + update
    spread = jax.nn.relu(jnp.dot(standardize_features(pair_mid, grid_scale_vector).astype(jnp.bfloat16), grid_widen_map, preferred_element_type=jnp.float32)).astype(jnp.bfloat16)
    grid_revised = pair_mid + jnp.dot(spread, grid_shrink_map, preferred_element_type=jnp.float32)
    return (alignment_revised, grid_revised)

def reference(alignment_tensor, residue_grid, mixing_scale_vector, logit_offset_scale, feedforward_scale, product_scale_vector, grid_scale_vector, logit_offset_map, asking_mapping, lookup_mapping, content_mapping, mixing_return_matrix, alignment_widen_map, alignment_shrink_map, former_embedding_map, latter_embedding_map, product_return_map, grid_widen_map, grid_shrink_map):
    alignment_samples = []
    grid_samples = []
    for sample_number in range(SAMPLE_TOTAL):
        former_embedding, latter_embedding = lone_sample(alignment_tensor[sample_number], residue_grid[sample_number], mixing_scale_vector, logit_offset_scale, feedforward_scale, product_scale_vector, grid_scale_vector, logit_offset_map, asking_mapping, lookup_mapping, content_mapping, mixing_return_matrix, alignment_widen_map, alignment_shrink_map, former_embedding_map, latter_embedding_map, product_return_map, grid_widen_map, grid_shrink_map)
        alignment_samples.append(former_embedding)
        grid_samples.append(latter_embedding)
    return (jnp.stack(alignment_samples), jnp.stack(grid_samples))
```

```python
import functools

import jax
import jax.numpy as jnp
from jax import lax
from jax.experimental import pallas as pl
from jax.experimental.pallas import tpu as pltpu
from jax.sharding import PartitionSpec as P

EPS = 1e-05
LANES = 128
LOG2E = 1.4426950408889634


def standardize_features(x, gain):
    mean = jnp.mean(x, axis=-1, keepdims=True)
    var = jnp.mean((x - mean) ** 2, axis=-1, keepdims=True)
    return (x - mean) * lax.rsqrt(var + EPS) * gain


def gathered(
    alignment_tensor,
    residue_grid,
    mixing_scale_vector,
    logit_offset_scale,
    feedforward_scale,
    product_scale_vector,
    grid_scale_vector,
    logit_offset_map,
    asking_mapping,
    lookup_mapping,
    content_mapping,
    mixing_return_matrix,
    alignment_widen_map,
    alignment_shrink_map,
    former_embedding_map,
    latter_embedding_map,
    product_return_map,
    grid_widen_map,
    grid_shrink_map,
):
    sample_alignment = alignment_tensor[0]
    local_pair = residue_grid[0]
    subspace_total = logit_offset_map.shape[1]
    feature_extent = sample_alignment.shape[-1]
    subspace_number = feature_extent // subspace_total
    sequences_available = sample_alignment.shape[0]
    chain_available = sample_alignment.shape[1]
    tile_rows = local_pair.shape[0]
    tile_cols = local_pair.shape[1]
    product_extent = former_embedding_map.shape[1]
    product_operands = standardize_features(sample_alignment, product_scale_vector).astype(
        jnp.bfloat16
    )
    former_tensor = jnp.dot(
        product_operands, former_embedding_map, preferred_element_type=jnp.float32
    ).astype(jnp.bfloat16)
    latter_tensor = jnp.dot(
        product_operands, latter_embedding_map, preferred_element_type=jnp.float32
    ).astype(jnp.bfloat16)
    left_rows, right_rows = (
        lax.all_gather(former_tensor, "tile", axis=0, tiled=True),
        lax.all_gather(latter_tensor, "tile", axis=0, tiled=True),
    )
    left_all = lax.all_gather(left_rows, "col", axis=1, tiled=True)
    left_mine = lax.dynamic_slice_in_dim(left_all, lax.axis_index("tile") * tile_rows, tile_rows, 1)
    tensor_product = (
        jnp.einsum("era,eyq->ryaq", left_mine, right_rows, preferred_element_type=jnp.float32)
        / left_rows.shape[0]
    )
    update = jnp.dot(
        tensor_product.reshape(tile_rows, tile_cols, product_extent * product_extent),
        product_return_map,
        precision=lax.Precision.HIGHEST,
    )
    bias_tile = jnp.einsum(
        "ijc,ch->hij",
        standardize_features(local_pair, logit_offset_scale),
        logit_offset_map,
        precision=lax.Precision.HIGHEST,
    )
    wide = lax.all_gather(bias_tile, "col", axis=2, tiled=True)
    whole = lax.all_gather(wide.astype(jnp.bfloat16), "tile", axis=1, tiled=True).astype(wide.dtype)
    bias = lax.dynamic_slice_in_dim(
        whole, lax.axis_index("col") * chain_available, chain_available, 1
    )
    standardized_source = standardize_features(sample_alignment, mixing_scale_vector).astype(
        jnp.bfloat16
    )
    asking_vectors = jnp.dot(
        standardized_source, asking_mapping, preferred_element_type=jnp.float32
    ).astype(jnp.bfloat16)
    lookup_vectors = jnp.dot(
        standardized_source, lookup_mapping, preferred_element_type=jnp.float32
    ).astype(jnp.bfloat16)
    content_vectors = jnp.dot(
        standardized_source, content_mapping, preferred_element_type=jnp.float32
    ).astype(jnp.bfloat16)
    all_keys, all_values = (
        lax.all_gather(lookup_vectors, "col", axis=1, tiled=True),
        lax.all_gather(content_vectors, "col", axis=1, tiled=True),
    )
    total_res = all_keys.shape[1]
    asking_vectors = asking_vectors.reshape(
        sequences_available, chain_available, subspace_total, subspace_number
    )
    all_keys = all_keys.reshape(sequences_available, total_res, subspace_total, subspace_number)
    all_values = all_values.reshape(sequences_available, total_res, subspace_total, subspace_number)
    scores = (
        jnp.einsum("sqhd,skhd->shqk", asking_vectors, all_keys, preferred_element_type=jnp.float32)
        / jnp.sqrt(jnp.float32(subspace_number))
        + bias[None]
    )
    weights = jax.nn.softmax(scores, axis=-1).astype(jnp.bfloat16)
    mixing_outcome = jnp.einsum(
        "shqk,skhd->sqhd", weights, all_values, preferred_element_type=jnp.float32
    )
    mixing_outcome = mixing_outcome.astype(jnp.bfloat16).reshape(
        sequences_available, chain_available, feature_extent
    )
    alignment_activations = sample_alignment + jnp.dot(
        mixing_outcome, mixing_return_matrix, preferred_element_type=jnp.float32
    )
    expanded_features = jax.nn.relu(
        jnp.dot(
            standardize_features(alignment_activations, feedforward_scale).astype(jnp.bfloat16),
            alignment_widen_map,
            preferred_element_type=jnp.float32,
        )
    ).astype(jnp.bfloat16)
    alignment_revised = alignment_activations + jnp.dot(
        expanded_features, alignment_shrink_map, preferred_element_type=jnp.float32
    )
    pair_mid = local_pair + update
    spread = jax.nn.relu(
        jnp.dot(
            standardize_features(pair_mid, grid_scale_vector).astype(jnp.bfloat16),
            grid_widen_map,
            preferred_element_type=jnp.float32,
        )
    ).astype(jnp.bfloat16)
    grid_revised = pair_mid + jnp.dot(spread, grid_shrink_map, preferred_element_type=jnp.float32)
    return (alignment_revised[None], grid_revised[None])


def normalized(x):
    mean = jnp.mean(x, axis=-1, keepdims=True)
    centered = x - mean
    var = jnp.mean(centered * centered, axis=-1, keepdims=True)
    return centered * lax.rsqrt(var + EPS)


def dot(a, b, dims=((1,), (0,))):
    return lax.dot_general(a, b, (dims, ((), ())), preferred_element_type=jnp.float32)


def factors_kernel(rows, x_ref, mix_ref, gain_ref, wl_ref, wr_ref, normed_ref, left_ref, right_ref, std, lacc, racc):
    step = pl.program_id(0)
    block, residues, features = x_ref.shape
    extent = wl_ref.shape[1]
    pack = LANES // extent
    groups = residues // pack
    base = normalized(x_ref[...].reshape(block * residues, features))
    normed_ref[...] = (base * mix_ref[...]).astype(jnp.bfloat16).reshape(block, residues, features)
    scaled = base * gain_ref[...]
    spans = features // LANES
    for f in range(spans):
        std[f] = scaled[:, f * LANES : (f + 1) * LANES]
    turned = dot(wr_ref[...], scaled.astype(jnp.bfloat16), ((0,), (1,)))
    packed = jnp.zeros((block * groups, LANES), jnp.float32)
    source = lax.broadcasted_iota(jnp.int32, (extent, LANES), 0)
    target = lax.broadcasted_iota(jnp.int32, (extent, LANES), 1)
    for a in range(pack):
        spread = (source + a * extent == target).astype(jnp.bfloat16)
        wide = dot(wl_ref[...], spread).astype(jnp.bfloat16)
        picked = [std[f, pl.ds(a, block * groups, stride=pack), :] for f in range(spans)]
        packed = packed + dot(jnp.concatenate(picked, axis=1).astype(jnp.bfloat16), wide)
    for k in range(block):
        row = step * block + k
        racc[pl.ds(row, extent, stride=rows), :] = turned[:, k * residues : (k + 1) * residues]
        lacc[pl.ds(row, groups, stride=rows), :] = packed[k * groups : (k + 1) * groups]

    @pl.when(step == pl.num_programs(0) - 1)
    def _():
        left_ref[...] = lacc[...].astype(jnp.bfloat16)
        right_ref[...] = racc[...].astype(jnp.bfloat16)


def factors(x, mix, gain, wl, wr, block):
    rows, residues, features = x.shape
    extent = wl.shape[1]
    groups = residues * extent // LANES
    whole = lambda shape: pl.BlockSpec(shape, lambda i: (0,) * len(shape))
    tile = pl.BlockSpec((block, residues, features), lambda i: (i, 0, 0))
    return pl.pallas_call(
        functools.partial(factors_kernel, rows),
        grid=(rows // block,),
        in_specs=[tile, whole((1, features)), whole((1, features)), whole(wl.shape), whole(wr.shape)],
        out_specs=[tile, whole((groups * rows, LANES)), whole((extent * rows, residues))],
        out_shape=[
            jax.ShapeDtypeStruct((rows, residues, features), jnp.bfloat16),
            jax.ShapeDtypeStruct((groups * rows, LANES), jnp.bfloat16),
            jax.ShapeDtypeStruct((extent * rows, residues), jnp.bfloat16),
        ],
        scratch_shapes=[
            pltpu.VMEM((features // LANES, block * residues, LANES), jnp.float32),
            pltpu.VMEM((groups * rows, LANES), jnp.float32),
            pltpu.VMEM((extent * rows, residues), jnp.float32),
        ],
        name="factors",
        cost_estimate=pl.CostEstimate(
            flops=2 * rows * residues * features * 5 * extent,
            bytes_accessed=rows * residues * features * 6,
            transcendentals=rows * residues,
        ),
    )(x, mix.reshape(1, -1), gain.reshape(1, -1), wl, wr)


def bias_kernel(heads, x_ref, gain_ref, w_ref, out_ref, acc):
    step = pl.program_id(0)
    block, cols, features = x_ref.shape
    rows = acc.shape[0] // heads
    scaled = normalized(x_ref[...].reshape(block * cols, features)) * gain_ref[...]
    turned = dot(w_ref[...].astype(jnp.bfloat16), scaled.astype(jnp.bfloat16), ((0,), (1,)))
    for k in range(block):
        acc[pl.ds(step * block + k, heads, stride=rows), :] = turned[:, k * cols : (k + 1) * cols]

    @pl.when(step == pl.num_programs(0) - 1)
    def _():
        out_ref[...] = acc[...].astype(jnp.bfloat16)


def pair_bias(pair, gain, w, block):
    rows, cols, features = pair.shape
    heads = w.shape[1]
    whole = lambda shape: pl.BlockSpec(shape, lambda i: (0,) * len(shape))
    return pl.pallas_call(
        functools.partial(bias_kernel, heads),
        grid=(rows // block,),
        in_specs=[
            pl.BlockSpec((block, cols, features), lambda i: (i, 0, 0)),
            whole((1, features)),
            whole(w.shape),
        ],
        out_specs=whole((heads * rows, cols)),
        out_shape=jax.ShapeDtypeStruct((heads * rows, cols), jnp.bfloat16),
        scratch_shapes=[pltpu.VMEM((heads * rows, cols), jnp.float32)],
        name="pair_bias",
        cost_estimate=pl.CostEstimate(
            flops=2 * rows * cols * features * heads * 8,
            bytes_accessed=rows * cols * features * 4,
            transcendentals=rows * cols,
        ),
    )(pair, gain.reshape(1, -1), w).reshape(heads, rows, cols)


def pair_kernel(parts, rows, extent, *refs):
    lefts, rights = refs[:parts], refs[parts : 2 * parts]
    pair_ref, wt_ref, gain_ref, wide_ref, shrink_ref, out_ref, rall, lall, outer = refs[2 * parts :]
    step = pl.program_id(0)
    block, cols, channels = pair_ref.shape

    @pl.when(step == 0)
    def _():
        for b, right in enumerate(rights):
            for d in range(extent):
                rall[b * rows : (b + 1) * rows, d * cols : (d + 1) * cols] = right[d * rows : (d + 1) * rows, :]
        for r in range(lefts[0].shape[0] // rows):
            stacked = jnp.concatenate([left[r * rows : (r + 1) * rows, :] for left in lefts], axis=0)
            lall[r * LANES : (r + 1) * LANES, :] = stacked.T

    mine = lall[pl.ds(pl.multiple_of(step * block * extent, block * extent), block * extent), :]
    chunk = min(8, extent)
    for d0 in range(0, extent, chunk):
        product = dot(mine, rall[:, d0 * cols : (d0 + chunk) * cols]).astype(jnp.bfloat16)
        for i in range(block):
            for d in range(chunk):
                outer[i // 2, (d0 + d) * extent : (d0 + d + 1) * extent, (i % 2) * cols : (i % 2 + 1) * cols] = product[
                    i * extent : (i + 1) * extent, d * cols : (d + 1) * cols
                ]
    for k in range(block // 2):
        turned = dot(wt_ref[...], outer[k])
        mids = []
        for i in range(2):
            mids.append(pair_ref[2 * k + i] + turned[:, i * cols : (i + 1) * cols].T)
        mid = jnp.concatenate(mids, axis=0)
        normed = (normalized(mid) * gain_ref[...]).astype(jnp.bfloat16)
        spread = jnp.maximum(dot(normed, wide_ref[...]), 0.0).astype(jnp.bfloat16)
        done = mid + dot(spread, shrink_ref[...])
        out_ref[2 * k : 2 * k + 2] = done.reshape(2, cols, channels)


def pair_update(lefts, rights, pair, wt, gain, wide, shrink, rows, block):
    parts = len(lefts)
    tile_rows, cols, channels = pair.shape
    extent = rights[0].shape[0] // rows
    whole = lambda shape: pl.BlockSpec(shape, lambda i: (0,) * len(shape))
    tile = pl.BlockSpec((block, cols, channels), lambda i: (i, 0, 0))
    return pl.pallas_call(
        functools.partial(pair_kernel, parts, rows, extent),
        grid=(tile_rows // block,),
        in_specs=[whole(a.shape) for a in (*lefts, *rights)]
        + [tile, whole(wt.shape), whole((1, channels)), whole(wide.shape), whole(shrink.shape)],
        out_specs=tile,
        out_shape=jax.ShapeDtypeStruct(pair.shape, jnp.float32),
        scratch_shapes=[
            pltpu.VMEM((parts * rows, extent * cols), jnp.bfloat16),
            pltpu.VMEM((tile_rows * extent, parts * rows), jnp.bfloat16),
            pltpu.VMEM((block // 2, extent * extent, 2 * cols), jnp.bfloat16),
        ],
        name="pair_update",
        cost_estimate=pl.CostEstimate(
            flops=2 * tile_rows * cols * (extent * extent * (parts * rows + channels) + 2 * wide.size) * 2,
            bytes_accessed=pair.size * 8,
            transcendentals=tile_rows * cols,
        ),
    )(*lefts, *rights, pair, wt, gain.reshape(1, -1), wide, shrink)


def attention_kernel(
    heads, where_ref, x_ref, own_ref, far_ref, b00, b01, b10, b11, wq_ref, wk_ref, wv_ref, wo_ref, gain_ref,
    wide_ref, shrink_ref, out_ref, bias,
):
    step = pl.program_id(0)
    block, residues, features = x_ref.shape
    depth = features // heads
    half = residues // 2
    bf16 = jnp.bfloat16

    @pl.when(step == 0)
    def _():
        first = pl.multiple_of(where_ref[0] * half, half)
        second = pl.multiple_of((1 - where_ref[0]) * half, half)
        for start, (near, far) in ((first, (b00, b01)), (second, (b10, b11))):
            bias[:, pl.ds(start, half), :residues] = near[...].astype(jnp.float32) * LOG2E
            bias[:, pl.ds(start, half), residues:] = far[...].astype(jnp.float32) * LOG2E

    x = x_ref[...].reshape(block * residues, features)
    own = own_ref[...].reshape(block * residues, features)
    far = far_ref[...].reshape(block * residues, features)
    factor = LOG2E / (depth**0.5)
    query = (dot(own, wq_ref[...]) * factor).astype(bf16)
    keys = [dot(a, wk_ref[...]).astype(bf16) for a in (own, far)]
    values = [dot(a, wv_ref[...]).astype(bf16) for a in (own, far)]
    lane = lax.broadcasted_iota(jnp.int32, (1, features), 1) // depth
    mixed = []
    for s in range(block):
        rows = slice(s * residues, (s + 1) * residues)
        key = jnp.concatenate([k[rows] for k in keys], axis=0)
        value = jnp.concatenate([v[rows] for v in values], axis=0)
        total = jnp.zeros((residues, features), jnp.float32)
        for h in range(heads):
            mask = lane == h
            only = query[rows] * mask.astype(bf16)
            score = dot(only, key, ((1,), (1,))) + bias[h]
            weight = jnp.exp2(score - jnp.max(score, axis=-1, keepdims=True))
            norm = 1.0 / jnp.sum(weight, axis=-1, keepdims=True)
            total = jnp.where(mask, dot(weight.astype(bf16), value) * norm, total)
        mixed.append(total.astype(bf16))
    mid = x + dot(jnp.concatenate(mixed, axis=0), wo_ref[...])
    normed = (normalized(mid) * gain_ref[...]).astype(bf16)
    lifted = jnp.maximum(dot(normed, wide_ref[...]), 0.0).astype(bf16)
    out_ref[...] = (mid + dot(lifted, shrink_ref[...])).reshape(block, residues, features)


def attention(parity, x, own, far, biases, weights, gain, wide, shrink, block):
    rows, residues, features = x.shape
    heads = biases[0].shape[0]
    whole = lambda shape: pl.BlockSpec(shape, lambda i, *_: (0,) * len(shape))
    tile = pl.BlockSpec((block, residues, features), lambda i, *_: (i, 0, 0))
    return pl.pallas_call(
        functools.partial(attention_kernel, heads),
        grid_spec=pltpu.PrefetchScalarGridSpec(
            num_scalar_prefetch=1,
            grid=(rows // block,),
            in_specs=[tile, tile, tile]
            + [whole(b.shape) for b in biases]
            + [whole(w.shape) for w in weights]
            + [whole((1, features)), whole(wide.shape), whole(shrink.shape)],
            out_specs=tile,
            scratch_shapes=[pltpu.VMEM((heads, residues, 2 * residues), jnp.float32)],
        ),
        out_shape=jax.ShapeDtypeStruct(x.shape, jnp.float32),
        name="attention",
        cost_estimate=pl.CostEstimate(
            flops=2 * rows * residues * (6 * features * features + 4 * heads * residues * features + 2 * wide.size),
            bytes_accessed=rows * residues * features * 12,
            transcendentals=rows * residues * heads * 2 * residues,
        ),
    )(parity, x, own, far, *biases, *weights, gain.reshape(1, -1), wide, shrink)


def exchanged(
    alignment_tensor,
    residue_grid,
    mixing_scale_vector,
    logit_offset_scale,
    feedforward_scale,
    product_scale_vector,
    grid_scale_vector,
    logit_offset_map,
    asking_mapping,
    lookup_mapping,
    content_mapping,
    mixing_return_matrix,
    alignment_widen_map,
    alignment_shrink_map,
    former_embedding_map,
    latter_embedding_map,
    product_return_map,
    grid_widen_map,
    grid_shrink_map,
):
    msa, pair = alignment_tensor[0], residue_grid[0]
    rows = msa.shape[0]
    tiles = lax.axis_size("tile")
    extent = former_embedding_map.shape[1]
    channels = pair.shape[-1]
    mine, side = lax.axis_index("tile"), lax.axis_index("col")
    upper = tiles // 2

    def swap(value, axis, mask):
        return lax.ppermute(value, axis, [(i, i ^ mask) for i in range(lax.axis_size(axis))])

    normed, left, right = factors(
        msa, mixing_scale_vector, product_scale_vector, former_embedding_map, latter_embedding_map, 4
    )
    left_far = swap(left, "col", 1)
    low = jnp.where(side == 0, left, left_far)
    high = jnp.where(side == 0, left_far, left)
    rights = [right] + [swap(right, "tile", k) for k in range(1, tiles)]
    pieces = jnp.concatenate([low, high], axis=0).reshape(tiles, -1, LANES)
    lefts = [lax.dynamic_index_in_dim(pieces, mine, 0, keepdims=False)]
    for k in range(1, tiles):
        lefts.append(swap(lax.dynamic_index_in_dim(pieces, mine ^ k, 0, keepdims=False), "tile", k))

    tile_bias = pair_bias(pair, logit_offset_scale, logit_offset_map, 8)
    other = swap(tile_bias, "tile", upper)
    stays = (mine // upper) == side
    near = jnp.where(stays, tile_bias, other)
    gone = jnp.where(stays, other, tile_bias)
    far = swap(gone, "col", 1)
    biases = (near, far, swap(near, "tile", 1), swap(far, "tile", 1))

    normed_far = swap(normed, "col", 1)

    total_rows = rows * tiles
    wt = product_return_map.reshape(extent, extent, channels).transpose(2, 1, 0).reshape(channels, extent * extent)
    wt = (wt * (1.0 / total_rows)).astype(jnp.bfloat16)
    grid_revised = pair_update(
        lefts, rights, pair, wt, grid_scale_vector, grid_widen_map, grid_shrink_map, rows, 8
    )
    parity = (mine % upper).astype(jnp.int32).reshape(1)
    alignment_revised = attention(
        parity,
        msa,
        normed,
        normed_far,
        biases,
        (asking_mapping, lookup_mapping, content_mapping, mixing_return_matrix),
        feedforward_scale,
        alignment_widen_map,
        alignment_shrink_map,
        2,
    )
    return (alignment_revised[None], grid_revised[None])


def on_device(*args):
    msa, pair = args[0], args[1]
    extent = args[14].shape[1]
    fits = (
        lax.axis_size("col") == 2
        and lax.axis_size("tile") == 4
        and msa.shape[1] % 16 == 0
        and msa.shape[2] == LANES
        and pair.shape[1] % 16 == 0
        and pair.shape[2] == LANES
        and LANES % extent == 0
        and extent % 16 == 0
    )
    return exchanged(*args) if fits else gathered(*args)


def solution(mesh):
    placed = (
        P(("groups", "branch"), "tile", "col", None),
        P(("groups", "branch"), "tile", "col", None),
        P(),
        P(),
        P(),
        P(),
        P(),
        P(),
        P(),
        P(),
        P(),
        P(),
        P(),
        P(),
        P(),
        P(),
        P(),
        P(),
        P(),
    )
    return jax.shard_map(
        on_device,
        mesh=mesh,
        in_specs=placed,
        out_specs=(
            P(("groups", "branch"), "tile", "col", None),
            P(("groups", "branch"), "tile", "col", None),
        ),
        check_vma=False,
    )
```

```python
import functools

import jax
import jax.numpy as jnp
from jax import lax
from jax.experimental import pallas as pl
from jax.experimental.pallas import tpu as pltpu
from jax.sharding import PartitionSpec as P


EPS = 1e-05
LANES = 128
LOG2E = 1.4426950408889634


def standardize_features(x, gain):
    mean = jnp.mean(x, axis=-1, keepdims=True)
    var = jnp.mean((x - mean) ** 2, axis=-1, keepdims=True)
    return (x - mean) * lax.rsqrt(var + EPS) * gain


def gathered(
    alignment_tensor,
    residue_grid,
    mixing_scale_vector,
    logit_offset_scale,
    feedforward_scale,
    product_scale_vector,
    grid_scale_vector,
    logit_offset_map,
    asking_mapping,
    lookup_mapping,
    content_mapping,
    mixing_return_matrix,
    alignment_widen_map,
    alignment_shrink_map,
    former_embedding_map,
    latter_embedding_map,
    product_return_map,
    grid_widen_map,
    grid_shrink_map,
):
    sample_alignment = alignment_tensor[0]
    local_pair = residue_grid[0]
    subspace_total = logit_offset_map.shape[1]
    feature_extent = sample_alignment.shape[-1]
    subspace_number = feature_extent // subspace_total
    sequences_available = sample_alignment.shape[0]
    chain_available = sample_alignment.shape[1]
    tile_rows = local_pair.shape[0]
    tile_cols = local_pair.shape[1]
    product_extent = former_embedding_map.shape[1]
    product_operands = standardize_features(sample_alignment, product_scale_vector).astype(
        jnp.bfloat16
    )
    former_tensor = jnp.dot(
        product_operands, former_embedding_map, preferred_element_type=jnp.float32
    ).astype(jnp.bfloat16)
    latter_tensor = jnp.dot(
        product_operands, latter_embedding_map, preferred_element_type=jnp.float32
    ).astype(jnp.bfloat16)
    left_rows, right_rows = (
        lax.all_gather(former_tensor, "tile", axis=0, tiled=True),
        lax.all_gather(latter_tensor, "tile", axis=0, tiled=True),
    )
    left_all = lax.all_gather(left_rows, "col", axis=1, tiled=True)
    left_mine = lax.dynamic_slice_in_dim(left_all, lax.axis_index("tile") * tile_rows, tile_rows, 1)
    tensor_product = (
        jnp.einsum("era,eyq->ryaq", left_mine, right_rows, preferred_element_type=jnp.float32)
        / left_rows.shape[0]
    )
    update = jnp.dot(
        tensor_product.reshape(tile_rows, tile_cols, product_extent * product_extent),
        product_return_map,
        precision=lax.Precision.HIGHEST,
    )
    bias_tile = jnp.einsum(
        "ijc,ch->hij",
        standardize_features(local_pair, logit_offset_scale),
        logit_offset_map,
        precision=lax.Precision.HIGHEST,
    )
    wide = lax.all_gather(bias_tile, "col", axis=2, tiled=True)
    whole = lax.all_gather(wide.astype(jnp.bfloat16), "tile", axis=1, tiled=True).astype(wide.dtype)
    bias = lax.dynamic_slice_in_dim(
        whole, lax.axis_index("col") * chain_available, chain_available, 1
    )
    standardized_source = standardize_features(sample_alignment, mixing_scale_vector).astype(
        jnp.bfloat16
    )
    asking_vectors = jnp.dot(
        standardized_source, asking_mapping, preferred_element_type=jnp.float32
    ).astype(jnp.bfloat16)
    lookup_vectors = jnp.dot(
        standardized_source, lookup_mapping, preferred_element_type=jnp.float32
    ).astype(jnp.bfloat16)
    content_vectors = jnp.dot(
        standardized_source, content_mapping, preferred_element_type=jnp.float32
    ).astype(jnp.bfloat16)
    all_keys, all_values = (
        lax.all_gather(lookup_vectors, "col", axis=1, tiled=True),
        lax.all_gather(content_vectors, "col", axis=1, tiled=True),
    )
    total_res = all_keys.shape[1]
    asking_vectors = asking_vectors.reshape(
        sequences_available, chain_available, subspace_total, subspace_number
    )
    all_keys = all_keys.reshape(sequences_available, total_res, subspace_total, subspace_number)
    all_values = all_values.reshape(sequences_available, total_res, subspace_total, subspace_number)
    scores = (
        jnp.einsum("sqhd,skhd->shqk", asking_vectors, all_keys, preferred_element_type=jnp.float32)
        / jnp.sqrt(jnp.float32(subspace_number))
        + bias[None]
    )
    weights = jax.nn.softmax(scores, axis=-1).astype(jnp.bfloat16)
    mixing_outcome = jnp.einsum(
        "shqk,skhd->sqhd", weights, all_values, preferred_element_type=jnp.float32
    )
    mixing_outcome = mixing_outcome.astype(jnp.bfloat16).reshape(
        sequences_available, chain_available, feature_extent
    )
    alignment_activations = sample_alignment + jnp.dot(
        mixing_outcome, mixing_return_matrix, preferred_element_type=jnp.float32
    )
    expanded_features = jax.nn.relu(
        jnp.dot(
            standardize_features(alignment_activations, feedforward_scale).astype(jnp.bfloat16),
            alignment_widen_map,
            preferred_element_type=jnp.float32,
        )
    ).astype(jnp.bfloat16)
    alignment_revised = alignment_activations + jnp.dot(
        expanded_features, alignment_shrink_map, preferred_element_type=jnp.float32
    )
    pair_mid = local_pair + update
    spread = jax.nn.relu(
        jnp.dot(
            standardize_features(pair_mid, grid_scale_vector).astype(jnp.bfloat16),
            grid_widen_map,
            preferred_element_type=jnp.float32,
        )
    ).astype(jnp.bfloat16)
    grid_revised = pair_mid + jnp.dot(spread, grid_shrink_map, preferred_element_type=jnp.float32)
    return (alignment_revised[None], grid_revised[None])


def normalized(x):
    mean = jnp.mean(x, axis=-1, keepdims=True)
    centered = x - mean
    var = jnp.mean(centered * centered, axis=-1, keepdims=True)
    return centered * lax.rsqrt(var + EPS)


def normalized_down(x):
    mean = jnp.mean(x, axis=0, keepdims=True)
    centered = x - mean
    var = jnp.mean(centered * centered, axis=0, keepdims=True)
    return centered * lax.rsqrt(var + EPS)


def down(row):
    return jnp.broadcast_to(row, (8, row.shape[1])).T[:, :1]


def dot(a, b, dims=((1,), (0,))):
    return lax.dot_general(a, b, (dims, ((), ())), preferred_element_type=jnp.float32)


def factors_kernel(rows, upper, x_ref, mix_ref, gain_ref, wl_ref, wr_ref, normed_ref, even_ref, odd_ref, right_ref, std, half_scaled, lacc, racc):
    step = pl.program_id(0)
    block, residues, features = x_ref.shape
    extent = wl_ref.shape[0]
    pack = LANES // extent
    groups = residues // pack
    spans = features // LANES
    source = lax.broadcasted_iota(jnp.int32, (extent, LANES), 0)
    target = lax.broadcasted_iota(jnp.int32, (extent, LANES), 1)
    wides = []
    for a in range(pack):
        spread = (source + a * extent == target).astype(jnp.bfloat16)
        wides.append(dot(wl_ref[...], spread, ((0,), (0,))).astype(jnp.bfloat16))
    for t in range(block + 1):
        if t < block:
            base = normalized(x_ref[t])
            normed_ref[t] = (base * mix_ref[...]).astype(jnp.bfloat16)
            scaled = base * gain_ref[...]
            for f in range(spans):
                std[t, f] = scaled[:, f * LANES : (f + 1) * LANES]
            half_scaled[t] = scaled.astype(jnp.bfloat16)
        if t >= 1:
            k = t - 1
            row = step * block + k
            racc[pl.ds(row, extent, stride=rows), :] = dot(wr_ref[...], half_scaled[k], ((1,), (1,)))
            packed = jnp.zeros((groups, LANES), jnp.float32)
            for a in range(pack):
                picked = [std[k, f, pl.ds(a, groups, stride=pack), :] for f in range(spans)]
                packed = packed + dot(jnp.concatenate(picked, axis=1).astype(jnp.bfloat16), wides[a])
            lacc[pl.ds(row, groups, stride=rows), :] = packed

    @pl.when(step == pl.num_programs(0) - 1)
    def _():
        size = even_ref.shape[0]
        at = lax.axis_index("tile") % upper
        for mask, ref in enumerate((even_ref, odd_ref)):
            ref[...] = lacc[pl.ds(pl.multiple_of((at ^ mask) * size, size), size), :].astype(jnp.bfloat16)
        right_ref[...] = racc[...].astype(jnp.bfloat16)


def factors(x, mix, gain, wl, wr, upper, block):
    rows, residues, features = x.shape
    extent = wl.shape[0]
    groups = residues * extent // LANES
    whole = lambda shape: pl.BlockSpec(shape, lambda i: (0,) * len(shape))
    tile = pl.BlockSpec((block, residues, features), lambda i: (i, 0, 0))
    return pl.pallas_call(
        functools.partial(factors_kernel, rows, upper),
        grid=(rows // block,),
        in_specs=[tile, whole((1, features)), whole((1, features)), whole(wl.shape), whole(wr.shape)],
        out_specs=[tile, *[whole((groups * rows // upper, LANES))] * 2, whole((extent * rows, residues))],
        out_shape=[
            jax.ShapeDtypeStruct((rows, residues, features), jnp.bfloat16),
            *[jax.ShapeDtypeStruct((groups * rows // upper, LANES), jnp.bfloat16)] * 2,
            jax.ShapeDtypeStruct((extent * rows, residues), jnp.bfloat16),
        ],
        scratch_shapes=[
            pltpu.VMEM((block, features // LANES, residues, LANES), jnp.float32),
            pltpu.VMEM((block, residues, features), jnp.bfloat16),
            pltpu.VMEM((groups * rows, LANES), jnp.float32),
            pltpu.VMEM((extent * rows, residues), jnp.float32),
        ],
        name="factors",
        cost_estimate=pl.CostEstimate(
            flops=2 * rows * residues * features * 5 * extent,
            bytes_accessed=rows * residues * features * 6,
            transcendentals=rows * residues,
        ),
    )(x, mix.reshape(1, -1), gain.reshape(1, -1), wl, wr)


def bias_kernel(heads, x_ref, gain_ref, w_ref, out_ref, acc):
    step = pl.program_id(0)
    block, _, _ = x_ref.shape
    rows = acc.shape[0] // heads
    w = w_ref[...].astype(jnp.bfloat16)
    gain = down(gain_ref[...])
    turned, scaled = {}, {}
    for t in range(block + 2):
        if t >= 2:
            acc[pl.ds(step * block + t - 2, heads, stride=rows), :] = dot(w, scaled.pop(t - 2))
        if t < block:
            turned[t] = x_ref[t].T
        if 1 <= t <= block:
            scaled[t - 1] = (normalized_down(turned.pop(t - 1)) * gain).astype(jnp.bfloat16)

    @pl.when(step == pl.num_programs(0) - 1)
    def _():
        out_ref[...] = acc[...].astype(jnp.bfloat16)


def pair_bias(pair, gain, w, block):
    rows, cols, features = pair.shape
    heads = w.shape[0]
    whole = lambda shape: pl.BlockSpec(shape, lambda i: (0,) * len(shape))
    return pl.pallas_call(
        functools.partial(bias_kernel, heads),
        grid=(rows // block,),
        in_specs=[
            pl.BlockSpec((block, cols, features), lambda i: (i, 0, 0)),
            whole((1, features)),
            whole(w.shape),
        ],
        out_specs=whole((heads * rows, cols)),
        out_shape=jax.ShapeDtypeStruct((heads * rows, cols), jnp.bfloat16),
        scratch_shapes=[pltpu.VMEM((heads * rows, cols), jnp.float32)],
        name="pair_bias",
        cost_estimate=pl.CostEstimate(
            flops=2 * rows * cols * features * heads * 8,
            bytes_accessed=rows * cols * features * 4,
            transcendentals=rows * cols,
        ),
    )(pair, gain.reshape(1, -1), w).reshape(heads, rows, cols)


def pair_kernel(masks, upper, rows, extent, *refs):
    parts = len(masks)
    lefts, rights = refs[:parts], refs[parts : 2 * parts]
    pair_ref, map_ref, gain_ref, wide_ref, shrink_ref, out_ref = refs[2 * parts : 2 * parts + 6]
    rall, lall, outer, maps, wt, wide_t, shrink_t, gains, middle, normed, hidden = refs[2 * parts + 6 :]
    step = pl.program_id(0)
    last = pl.num_programs(0) - 1
    block, cols, _ = pair_ref.shape
    bf16 = jnp.bfloat16

    @pl.when(step == 0)
    def _():
        tile = lax.axis_index("tile")
        crossed = (tile // upper != lax.axis_index("col")).astype(jnp.int32) * upper
        for mask, right in zip(masks, rights):
            start = pl.multiple_of((crossed ^ mask) * rows, rows)
            for d in range(extent):
                rall[pl.ds(start, rows), d * cols : (d + 1) * cols] = right[d * rows : (d + 1) * rows, :]
        for r in range(lefts[0].shape[0] // rows):
            stacked = jnp.concatenate([left[r * rows : (r + 1) * rows, :] for left in lefts], axis=0)
            lall[r * LANES : (r + 1) * LANES, :] = stacked.T
        for d in range(extent):
            picked = map_ref[pl.ds(d, extent, stride=extent), :] * (1.0 / (parts * rows))
            maps[d * extent : (d + 1) * extent, :] = picked
        wt[...] = maps[...].T.astype(bf16)
        wide_t[...] = wide_ref[...].T
        shrink_t[...] = shrink_ref[...].T
        gains[...] = jnp.broadcast_to(down(gain_ref[...]), gains.shape)

    fresh, ready = step % 2, (step + 1) % 2
    duo = 2
    size = block * extent
    first = pl.multiple_of(jnp.minimum(step, last - 1) * size, size)

    heights = 2 if block % 4 == 0 else 1
    height = block // heights

    def product(n):
        c, v = n // heights, n % heights
        lanes = slice(c * duo * cols, (c + 1) * duo * cols)
        start = pl.multiple_of(first + v * height * extent, height * extent)
        made = dot(lall[pl.ds(start, height * extent), :], rall[:, lanes]).astype(bf16)
        for i in range(height):
            row = v * height + i
            for d in range(duo):
                at = (c * duo + d) * extent
                outer[fresh, row // 2, at : at + extent, row % 2 * cols : (row % 2 + 1) * cols] = made[
                    i * extent : (i + 1) * extent, d * cols : (d + 1) * cols
                ]

    def update(k):
        mid = dot(wt[...], outer[ready, k])
        middle[k] = mid + jnp.concatenate([pair_ref[2 * k].T, pair_ref[2 * k + 1].T], axis=1)

    def scale(k):
        normed[k] = (normalized_down(middle[k]) * gains[...]).astype(bf16)

    split = hidden.shape[1] // 2

    def widen(c, k):
        at = slice(c * split, (c + 1) * split)
        hidden[k, at, :] = jnp.maximum(dot(wide_t[at, :], normed[k]), 0.0).astype(bf16)

    def shrink(k):
        done = middle[k] + dot(shrink_t[...], hidden[k])
        for i in range(2):
            out_ref[2 * k + i] = done[:, i * cols : (i + 1) * cols].T

    pairs = block // 2
    stages = (
        (0, update),
        (1, scale),
        (2, functools.partial(widen, 0)),
        (2, functools.partial(widen, 1)),
        (3, shrink),
    )
    feed = []
    for t in range(pairs + 3):
        for lag, stage in stages:
            if 0 <= t - lag < pairs:
                feed.append(functools.partial(stage, t - lag))
    chunks = extent // duo * heights

    @pl.when(step == 0)
    def _():
        for c in range(chunks):
            product(c)

    @pl.when((step > 0) & (step < last))
    def _():
        for n, piece in enumerate(feed):
            for c in range(n * chunks // len(feed), (n + 1) * chunks // len(feed)):
                product(c)
            piece()

    @pl.when(step == last)
    def _():
        for piece in feed:
            piece()


def pair_update(lefts, rights, masks, upper, pair, maps, gain, wide, shrink, rows, block):
    parts = len(lefts)
    tile_rows, cols, channels = pair.shape
    extent = rights[0].shape[0] // rows
    pairs = block // 2
    whole = lambda shape: pl.BlockSpec(shape, lambda i: (0,) * len(shape))
    tile = pl.BlockSpec((block, cols, channels), lambda i: (jnp.maximum(i - 1, 0), 0, 0))
    return pl.pallas_call(
        functools.partial(pair_kernel, masks, upper, rows, extent),
        grid=(tile_rows // block + 1,),
        in_specs=[whole(a.shape) for a in (*lefts, *rights)]
        + [tile, whole(maps.shape), whole((1, channels)), whole(wide.shape), whole(shrink.shape)],
        out_specs=tile,
        out_shape=jax.ShapeDtypeStruct(pair.shape, jnp.float32),
        scratch_shapes=[
            pltpu.VMEM((parts * rows, extent * cols), jnp.bfloat16),
            pltpu.VMEM((tile_rows * extent, parts * rows), jnp.bfloat16),
            pltpu.VMEM((2, pairs, extent * extent, 2 * cols), jnp.bfloat16),
            pltpu.VMEM((extent * extent, channels), jnp.float32),
            pltpu.VMEM((channels, extent * extent), jnp.bfloat16),
            pltpu.VMEM(wide.shape[::-1], jnp.bfloat16),
            pltpu.VMEM(shrink.shape[::-1], jnp.bfloat16),
            pltpu.VMEM((channels, 2 * cols), jnp.float32),
            pltpu.VMEM((pairs, channels, 2 * cols), jnp.float32),
            pltpu.VMEM((pairs, channels, 2 * cols), jnp.bfloat16),
            pltpu.VMEM((pairs, wide.shape[1], 2 * cols), jnp.bfloat16),
        ],
        name="pair_update",
        cost_estimate=pl.CostEstimate(
            flops=2 * tile_rows * cols * (extent * extent * (parts * rows + channels) + 2 * wide.size) * 2,
            bytes_accessed=pair.size * 8,
            transcendentals=tile_rows * cols,
        ),
    )(*lefts, *rights, pair, maps, gain.reshape(1, -1), wide, shrink)


def attention_kernel(
    heads, cols, x_ref, own_ref, far_ref, b0, b1, b2, b3, wq_ref, wk_ref, wv_ref, wo_ref, gain_ref, wide_ref,
    shrink_ref, out_ref, bias, natural, wq, wv, wo, wide_t, shrink_t, gains, masked, keys, values, score, weight,
    attended, middle, normed, hidden,
):
    step = pl.program_id(0)
    block, residues, features = x_ref.shape
    depth = features // heads
    half = residues // 2
    bf16 = jnp.bfloat16
    group = LANES // depth
    pairs = heads // 2
    units = block * pairs
    sides = features // LANES

    @pl.when(step == 0)
    def _():
        for h in range(heads):
            for r, tile in enumerate((b0, b1, b2, b3)):
                source = lax.axis_index("tile") ^ r
                top = pl.multiple_of(source // cols * half, half)
                edge = pl.multiple_of((source % cols ^ lax.axis_index("col")) * residues, residues)
                natural[pl.ds(top, half), pl.ds(edge, residues)] = tile[h].astype(jnp.float32) * LOG2E
            for side in range(2):
                bias[h // 2, side * residues : (side + 1) * residues, (h % 2) * residues : (h % 2 + 1) * residues] = (
                    natural[:, side * residues : (side + 1) * residues].T
                )
        for turned, ref in ((wq, wq_ref), (wv, wv_ref), (wo, wo_ref), (wide_t, wide_ref), (shrink_t, shrink_ref)):
            turned[...] = ref[...].T
        gains[...] = jnp.broadcast_to(down(gain_ref[...]), gains.shape)
        masked[...] = jnp.zeros_like(masked)
        for u in range(units):
            values[u, 2 * depth :, :] = jnp.ones((16, 2 * residues), bf16)

    def project():
        factor = LOG2E / (depth**0.5)
        own = own_ref[...].reshape(block * residues, features)
        far = far_ref[...].reshape(block * residues, features)
        query = (dot(wq[...], own, ((1,), (1,))) * factor).astype(bf16)
        for s in range(block):
            for h in range(heads):
                masked[
                    s * pairs + h // 2, h % group * depth : (h % group + 1) * depth, h % 2 * residues : (h % 2 + 1) * residues
                ] = query[h * depth : (h + 1) * depth, s * residues : (s + 1) * residues]
        for side, rows in enumerate((own, far)):
            key = dot(rows, wk_ref[...]).astype(bf16)
            value = dot(wv[...], rows, ((1,), (1,))).astype(bf16)
            for s in range(block):
                at = slice(s * residues, (s + 1) * residues)
                for f in range(sides):
                    keys[s, f, side * residues : (side + 1) * residues, :] = key[at, f * LANES : (f + 1) * LANES]
                for g in range(pairs):
                    values[s * pairs + g, : 2 * depth, side * residues : (side + 1) * residues] = value[
                        2 * g * depth : 2 * (g + 1) * depth, at
                    ]

    def stand():
        mid = x_ref[...].reshape(block * residues, features).T + dot(wo[...], attended[...])
        middle[...] = mid
        normed[...] = (normalized_down(mid) * gains[...]).astype(bf16)

    widths = 16
    chunk = hidden.shape[0] // widths
    part = features // 2

    def widen(c):
        at = slice(c * chunk, (c + 1) * chunk)
        hidden[at, :] = jnp.maximum(dot(wide_t[at, :], normed[...]), 0.0).astype(bf16)

    def shrink(c):
        at = slice(c * part, (c + 1) * part)
        done = middle[at, :] + dot(shrink_t[at, :], hidden[...])
        out_ref[:, :, at] = done.T.reshape(block, residues, part)

    feed = [functools.partial(widen, c) for c in range(widths)] + [functools.partial(shrink, c) for c in range(2)]

    def scores(u, i):
        s, g = u // pairs, u % pairs
        at = slice(i * residues, (i + 1) * residues)
        score[u % 2, at, :] = dot(keys[s, 2 * g // group, at, :], masked[u]) + bias[g, at, :]

    def soften(u, i):
        lanes = slice(i * residues, (i + 1) * residues)
        now = score[u % 2, :, lanes]
        weight[u % 2, :, lanes] = jnp.exp2(now - jnp.max(now, axis=0, keepdims=True)).astype(bf16)

    def attend(u):
        s, g = u // pairs, u % pairs
        out = dot(values[u], weight[u % 2])
        norm = 1.0 / out[2 * depth : 2 * depth + 1, :]
        for i in range(2):
            lanes = slice(i * residues, (i + 1) * residues)
            attended[(2 * g + i) * depth : (2 * g + i + 1) * depth, s * residues : (s + 1) * residues] = (
                out[i * depth : (i + 1) * depth, lanes] * norm[:, lanes]
            ).astype(bf16)

    def mix(left):
        for t in range(units + 2):
            for i in range(2):
                if i == 0 and t >= 2:
                    attend(t - 2)
                if t < units:
                    scores(t, i)
                if left:
                    left.pop(0)()
                if 1 <= t <= units:
                    soften(t - 1, i)

    @pl.when(step == 0)
    def _():
        project()
        mix([])

    @pl.when((step > 0) & (step < pl.num_programs(0) - 1))
    def _():
        stand()
        project()
        mix(list(feed))

    @pl.when(step == pl.num_programs(0) - 1)
    def _():
        stand()
        for piece in feed:
            piece()


def attention(cols, x, own, far, biases, weights, gain, wide, shrink, block):
    rows, residues, features = x.shape
    heads = biases[0].shape[0]
    depth = features // heads
    units = block * heads // 2
    steps = rows // block
    wide_residues = 2 * residues
    whole = lambda shape: pl.BlockSpec(shape, lambda i: (0,) * len(shape))
    tile = pl.BlockSpec((block, residues, features), lambda i: (jnp.minimum(i, steps - 1), 0, 0))
    late = pl.BlockSpec((block, residues, features), lambda i: (jnp.maximum(i - 1, 0), 0, 0))
    return pl.pallas_call(
        functools.partial(attention_kernel, heads, cols),
        grid=(steps + 1,),
        in_specs=[late, tile, tile]
        + [whole(b.shape) for b in biases]
        + [whole(w.shape) for w in weights]
        + [whole((1, features)), whole(wide.shape), whole(shrink.shape)],
        out_specs=late,
        scratch_shapes=[
            pltpu.VMEM((heads // 2, wide_residues, wide_residues), jnp.float32),
            pltpu.VMEM((residues, wide_residues), jnp.float32),
            *[pltpu.VMEM((features, features), jnp.bfloat16)] * 3,
            pltpu.VMEM(wide.shape[::-1], jnp.bfloat16),
            pltpu.VMEM(shrink.shape[::-1], jnp.bfloat16),
            pltpu.VMEM((features, block * residues), jnp.float32),
            pltpu.VMEM((units, LANES, wide_residues), jnp.bfloat16),
            pltpu.VMEM((block, features // LANES, wide_residues, LANES), jnp.bfloat16),
            pltpu.VMEM((units, 2 * depth + 16, wide_residues), jnp.bfloat16),
            pltpu.VMEM((2, wide_residues, wide_residues), jnp.float32),
            pltpu.VMEM((2, wide_residues, wide_residues), jnp.bfloat16),
            pltpu.VMEM((features, block * residues), jnp.bfloat16),
            pltpu.VMEM((features, block * residues), jnp.float32),
            pltpu.VMEM((features, block * residues), jnp.bfloat16),
            pltpu.VMEM((wide.shape[1], block * residues), jnp.bfloat16),
        ],
        out_shape=jax.ShapeDtypeStruct(x.shape, jnp.float32),
        name="attention",
        cost_estimate=pl.CostEstimate(
            flops=2 * rows * residues * (6 * features * features + 4 * heads * residues * features + 2 * wide.size),
            bytes_accessed=rows * residues * features * 12,
            transcendentals=rows * residues * heads * 2 * residues,
        ),
    )(x, own, far, *biases, *weights, gain.reshape(1, -1), wide, shrink)


def exchanged(
    alignment_tensor,
    residue_grid,
    mixing_scale_vector,
    logit_offset_scale,
    feedforward_scale,
    product_scale_vector,
    grid_scale_vector,
    logit_offset_map,
    asking_mapping,
    lookup_mapping,
    content_mapping,
    mixing_return_matrix,
    alignment_widen_map,
    alignment_shrink_map,
    former_embedding_map,
    latter_embedding_map,
    product_return_map,
    grid_widen_map,
    grid_shrink_map,
):
    msa, pair = alignment_tensor[0], residue_grid[0]
    rows = msa.shape[0]
    tiles = lax.axis_size("tile")
    upper = tiles // 2

    def swap(value, axis, mask):
        return lax.ppermute(value, axis, [(i, i ^ mask) for i in range(lax.axis_size(axis))])

    cols = lax.axis_size("col")
    normed, even, odd, right = factors(
        msa,
        mixing_scale_vector,
        product_scale_vector,
        former_embedding_map.T,
        latter_embedding_map.T,
        upper,
        min(rows, 8),
    )
    devices = [(t, c) for t in range(tiles) for c in range(cols)]

    def route(value, goal):
        pairs = [(t * cols + c, goal(t, c)[0] * cols + goal(t, c)[1]) for t, c in devices]
        return lax.ppermute(value, ("tile", "col"), pairs)

    def owner(r):
        def goal(t, c):
            aim = t ^ r
            return (aim, c) if aim // upper == c else (aim ^ upper, 1 - c)

        return goal

    right_up = swap(right, "tile", upper)
    lefts = []
    for r in range(tiles):
        lefts.append(route(odd if r % upper else even, owner(r)))
    right_side = swap(right, "tile", 1)
    normed_far = swap(normed, "col", 1)

    pair, _ = lax.optimization_barrier((pair, right))
    tile_bias = pair_bias(pair, logit_offset_scale, logit_offset_map.T, min(pair.shape[0], 32))
    tile_bias, right_up = lax.optimization_barrier((tile_bias, right_up))
    rights = [right, right_up, right_side, swap(right_up, "tile", 1)]
    masks = (0, upper, 1, upper + 1)
    biases = [
        route(tile_bias, lambda t, c, r=r: ((t % upper * cols + c) ^ r, t // upper)) for r in range(tiles)
    ]

    grid_revised = pair_update(
        lefts, rights, masks, upper, pair, product_return_map, grid_scale_vector, grid_widen_map, grid_shrink_map, rows, 16
    )
    alignment_revised = attention(
        cols,
        msa,
        normed,
        normed_far,
        biases,
        (asking_mapping, lookup_mapping, content_mapping, mixing_return_matrix),
        feedforward_scale,
        alignment_widen_map,
        alignment_shrink_map,
        2,
    )
    return (alignment_revised[None], grid_revised[None])


def on_device(*args):
    msa, pair = args[0], args[1]
    extent = args[14].shape[1]
    fits = (
        lax.axis_size("col") == 2
        and lax.axis_size("tile") == 4
        and msa.shape[1] % 16 == 0
        and msa.shape[2] == LANES
        and pair.shape[1] % 16 == 0
        and pair.shape[2] == LANES
        and LANES % extent == 0
        and extent % 16 == 0
    )
    if not fits:
        return gathered(*args)
    return exchanged(*args)


def solution(mesh):
    placed = (
        P(("groups", "branch"), "tile", "col", None),
        P(("groups", "branch"), "tile", "col", None),
        P(),
        P(),
        P(),
        P(),
        P(),
        P(),
        P(),
        P(),
        P(),
        P(),
        P(),
        P(),
        P(),
        P(),
        P(),
        P(),
        P(),
    )
    return jax.shard_map(
        on_device,
        mesh=mesh,
        in_specs=placed,
        out_specs=(
            P(("groups", "branch"), "tile", "col", None),
            P(("groups", "branch"), "tile", "col", None),
        ),
        check_vma=False,
    )
```

```python
import functools

import jax
import jax.numpy as jnp
from jax import lax
from jax.experimental import pallas as pl
from jax.experimental.pallas import tpu as pltpu
from jax.sharding import PartitionSpec as P


EPS = 1e-05
LANES = 128
LOG2E = 1.4426950408889634


def standardize_features(x, gain):
    mean = jnp.mean(x, axis=-1, keepdims=True)
    var = jnp.mean((x - mean) ** 2, axis=-1, keepdims=True)
    return (x - mean) * lax.rsqrt(var + EPS) * gain


def gathered(
    alignment_tensor,
    residue_grid,
    mixing_scale_vector,
    logit_offset_scale,
    feedforward_scale,
    product_scale_vector,
    grid_scale_vector,
    logit_offset_map,
    asking_mapping,
    lookup_mapping,
    content_mapping,
    mixing_return_matrix,
    alignment_widen_map,
    alignment_shrink_map,
    former_embedding_map,
    latter_embedding_map,
    product_return_map,
    grid_widen_map,
    grid_shrink_map,
):
    sample_alignment = alignment_tensor[0]
    local_pair = residue_grid[0]
    subspace_total = logit_offset_map.shape[1]
    feature_extent = sample_alignment.shape[-1]
    subspace_number = feature_extent // subspace_total
    sequences_available = sample_alignment.shape[0]
    chain_available = sample_alignment.shape[1]
    tile_rows = local_pair.shape[0]
    tile_cols = local_pair.shape[1]
    product_extent = former_embedding_map.shape[1]
    product_operands = standardize_features(sample_alignment, product_scale_vector).astype(
        jnp.bfloat16
    )
    former_tensor = jnp.dot(
        product_operands, former_embedding_map, preferred_element_type=jnp.float32
    ).astype(jnp.bfloat16)
    latter_tensor = jnp.dot(
        product_operands, latter_embedding_map, preferred_element_type=jnp.float32
    ).astype(jnp.bfloat16)
    left_rows, right_rows = (
        lax.all_gather(former_tensor, "tile", axis=0, tiled=True),
        lax.all_gather(latter_tensor, "tile", axis=0, tiled=True),
    )
    left_all = lax.all_gather(left_rows, "col", axis=1, tiled=True)
    left_mine = lax.dynamic_slice_in_dim(left_all, lax.axis_index("tile") * tile_rows, tile_rows, 1)
    tensor_product = (
        jnp.einsum("era,eyq->ryaq", left_mine, right_rows, preferred_element_type=jnp.float32)
        / left_rows.shape[0]
    )
    update = jnp.dot(
        tensor_product.reshape(tile_rows, tile_cols, product_extent * product_extent),
        product_return_map,
        precision=lax.Precision.HIGHEST,
    )
    bias_tile = jnp.einsum(
        "ijc,ch->hij",
        standardize_features(local_pair, logit_offset_scale),
        logit_offset_map,
        precision=lax.Precision.HIGHEST,
    )
    wide = lax.all_gather(bias_tile, "col", axis=2, tiled=True)
    whole = lax.all_gather(wide.astype(jnp.bfloat16), "tile", axis=1, tiled=True).astype(wide.dtype)
    bias = lax.dynamic_slice_in_dim(
        whole, lax.axis_index("col") * chain_available, chain_available, 1
    )
    standardized_source = standardize_features(sample_alignment, mixing_scale_vector).astype(
        jnp.bfloat16
    )
    asking_vectors = jnp.dot(
        standardized_source, asking_mapping, preferred_element_type=jnp.float32
    ).astype(jnp.bfloat16)
    lookup_vectors = jnp.dot(
        standardized_source, lookup_mapping, preferred_element_type=jnp.float32
    ).astype(jnp.bfloat16)
    content_vectors = jnp.dot(
        standardized_source, content_mapping, preferred_element_type=jnp.float32
    ).astype(jnp.bfloat16)
    all_keys, all_values = (
        lax.all_gather(lookup_vectors, "col", axis=1, tiled=True),
        lax.all_gather(content_vectors, "col", axis=1, tiled=True),
    )
    total_res = all_keys.shape[1]
    asking_vectors = asking_vectors.reshape(
        sequences_available, chain_available, subspace_total, subspace_number
    )
    all_keys = all_keys.reshape(sequences_available, total_res, subspace_total, subspace_number)
    all_values = all_values.reshape(sequences_available, total_res, subspace_total, subspace_number)
    scores = (
        jnp.einsum("sqhd,skhd->shqk", asking_vectors, all_keys, preferred_element_type=jnp.float32)
        / jnp.sqrt(jnp.float32(subspace_number))
        + bias[None]
    )
    weights = jax.nn.softmax(scores, axis=-1).astype(jnp.bfloat16)
    mixing_outcome = jnp.einsum(
        "shqk,skhd->sqhd", weights, all_values, preferred_element_type=jnp.float32
    )
    mixing_outcome = mixing_outcome.astype(jnp.bfloat16).reshape(
        sequences_available, chain_available, feature_extent
    )
    alignment_activations = sample_alignment + jnp.dot(
        mixing_outcome, mixing_return_matrix, preferred_element_type=jnp.float32
    )
    expanded_features = jax.nn.relu(
        jnp.dot(
            standardize_features(alignment_activations, feedforward_scale).astype(jnp.bfloat16),
            alignment_widen_map,
            preferred_element_type=jnp.float32,
        )
    ).astype(jnp.bfloat16)
    alignment_revised = alignment_activations + jnp.dot(
        expanded_features, alignment_shrink_map, preferred_element_type=jnp.float32
    )
    pair_mid = local_pair + update
    spread = jax.nn.relu(
        jnp.dot(
            standardize_features(pair_mid, grid_scale_vector).astype(jnp.bfloat16),
            grid_widen_map,
            preferred_element_type=jnp.float32,
        )
    ).astype(jnp.bfloat16)
    grid_revised = pair_mid + jnp.dot(spread, grid_shrink_map, preferred_element_type=jnp.float32)
    return (alignment_revised[None], grid_revised[None])


def normalized(x):
    mean = jnp.mean(x, axis=-1, keepdims=True)
    centered = x - mean
    var = jnp.mean(centered * centered, axis=-1, keepdims=True)
    return centered * lax.rsqrt(var + EPS)


def normalized_down(x):
    mean = jnp.mean(x, axis=0, keepdims=True)
    centered = x - mean
    var = jnp.mean(centered * centered, axis=0, keepdims=True)
    return centered * lax.rsqrt(var + EPS)


def down(row):
    return jnp.broadcast_to(row, (8, row.shape[1])).T[:, :1]


def dot(a, b, dims=((1,), (0,))):
    return lax.dot_general(a, b, (dims, ((), ())), preferred_element_type=jnp.float32)


def factors_kernel(rows, upper, x_ref, mix_ref, gain_ref, wl_ref, wr_ref, normed_ref, even_ref, odd_ref, right_ref, std, half_scaled, lacc, racc):
    step = pl.program_id(0)
    block, residues, features = x_ref.shape
    extent = wl_ref.shape[0]
    pack = LANES // extent
    groups = residues // pack
    spans = features // LANES
    source = lax.broadcasted_iota(jnp.int32, (extent, LANES), 0)
    target = lax.broadcasted_iota(jnp.int32, (extent, LANES), 1)
    wides = []
    for a in range(pack):
        spread = (source + a * extent == target).astype(jnp.bfloat16)
        wides.append(dot(wl_ref[...], spread, ((0,), (0,))).astype(jnp.bfloat16))
    for t in range(block + 1):
        if t < block:
            base = normalized(x_ref[t])
            normed_ref[t] = (base * mix_ref[...]).astype(jnp.bfloat16)
            scaled = base * gain_ref[...]
            for f in range(spans):
                std[t, f] = scaled[:, f * LANES : (f + 1) * LANES]
            half_scaled[t] = scaled.astype(jnp.bfloat16)
        if t >= 1:
            k = t - 1
            row = step * block + k
            racc[pl.ds(row, extent, stride=rows), :] = dot(wr_ref[...], half_scaled[k], ((1,), (1,)))
            packed = jnp.zeros((groups, LANES), jnp.float32)
            for a in range(pack):
                picked = [std[k, f, pl.ds(a, groups, stride=pack), :] for f in range(spans)]
                packed = packed + dot(jnp.concatenate(picked, axis=1).astype(jnp.bfloat16), wides[a])
            lacc[pl.ds(row, groups, stride=rows), :] = packed

    @pl.when(step == pl.num_programs(0) - 1)
    def _():
        size = even_ref.shape[0]
        at = lax.axis_index("tile") % upper
        for mask, ref in enumerate((even_ref, odd_ref)):
            ref[...] = lacc[pl.ds(pl.multiple_of((at ^ mask) * size, size), size), :].astype(jnp.bfloat16)
        right_ref[...] = racc[...].astype(jnp.bfloat16)


def factors(x, mix, gain, wl, wr, upper, block):
    rows, residues, features = x.shape
    extent = wl.shape[0]
    groups = residues * extent // LANES
    whole = lambda shape: pl.BlockSpec(shape, lambda i: (0,) * len(shape))
    tile = pl.BlockSpec((block, residues, features), lambda i: (i, 0, 0))
    return pl.pallas_call(
        functools.partial(factors_kernel, rows, upper),
        grid=(rows // block,),
        in_specs=[tile, whole((1, features)), whole((1, features)), whole(wl.shape), whole(wr.shape)],
        out_specs=[tile, *[whole((groups * rows // upper, LANES))] * 2, whole((extent * rows, residues))],
        out_shape=[
            jax.ShapeDtypeStruct((rows, residues, features), jnp.bfloat16),
            *[jax.ShapeDtypeStruct((groups * rows // upper, LANES), jnp.bfloat16)] * 2,
            jax.ShapeDtypeStruct((extent * rows, residues), jnp.bfloat16),
        ],
        scratch_shapes=[
            pltpu.VMEM((block, features // LANES, residues, LANES), jnp.float32),
            pltpu.VMEM((block, residues, features), jnp.bfloat16),
            pltpu.VMEM((groups * rows, LANES), jnp.float32),
            pltpu.VMEM((extent * rows, residues), jnp.float32),
        ],
        name="factors",
        cost_estimate=pl.CostEstimate(
            flops=2 * rows * residues * features * 5 * extent,
            bytes_accessed=rows * residues * features * 6,
            transcendentals=rows * residues,
        ),
    )(x, mix.reshape(1, -1), gain.reshape(1, -1), wl, wr)


def bias_kernel(heads, x_ref, gain_ref, w_ref, out_ref, acc):
    step = pl.program_id(0)
    block, _, _ = x_ref.shape
    rows = acc.shape[0] // heads
    w = w_ref[...].astype(jnp.bfloat16)
    gain = down(gain_ref[...])
    turned, scaled = {}, {}
    for t in range(block + 2):
        if t >= 2:
            acc[pl.ds(step * block + t - 2, heads, stride=rows), :] = dot(w, scaled.pop(t - 2))
        if t < block:
            turned[t] = x_ref[t].T
        if 1 <= t <= block:
            scaled[t - 1] = (normalized_down(turned.pop(t - 1)) * gain).astype(jnp.bfloat16)

    @pl.when(step == pl.num_programs(0) - 1)
    def _():
        out_ref[...] = acc[...].astype(jnp.bfloat16)


def pair_bias(pair, gain, w, block):
    rows, cols, features = pair.shape
    heads = w.shape[0]
    whole = lambda shape: pl.BlockSpec(shape, lambda i: (0,) * len(shape))
    return pl.pallas_call(
        functools.partial(bias_kernel, heads),
        grid=(rows // block,),
        in_specs=[
            pl.BlockSpec((block, cols, features), lambda i: (i, 0, 0)),
            whole((1, features)),
            whole(w.shape),
        ],
        out_specs=whole((heads * rows, cols)),
        out_shape=jax.ShapeDtypeStruct((heads * rows, cols), jnp.bfloat16),
        scratch_shapes=[pltpu.VMEM((heads * rows, cols), jnp.float32)],
        name="pair_bias",
        cost_estimate=pl.CostEstimate(
            flops=2 * rows * cols * features * heads * 8,
            bytes_accessed=rows * cols * features * 4,
            transcendentals=rows * cols,
        ),
    )(pair, gain.reshape(1, -1), w).reshape(heads, rows, cols)


def pair_kernel(masks, upper, rows, extent, *refs):
    parts = len(masks)
    lefts, rights = refs[:parts], refs[parts : 2 * parts]
    pair_ref, map_ref, gain_ref, wide_ref, shrink_ref, out_ref = refs[2 * parts : 2 * parts + 6]
    rall, lall, outer_a, outer_b, maps, wt, wide_t, shrink_t, gains, middle, normed, hidden = refs[2 * parts + 6 :]
    step = pl.program_id(0)
    last = pl.num_programs(0) - 1
    block, cols, _ = pair_ref.shape
    bf16 = jnp.bfloat16

    @pl.when(step == 0)
    def _():
        tile = lax.axis_index("tile")
        crossed = (tile // upper != lax.axis_index("col")).astype(jnp.int32) * upper
        for mask, right in zip(masks, rights):
            start = pl.multiple_of((crossed ^ mask) * rows, rows)
            for d in range(extent):
                rall[pl.ds(start, rows), d * cols : (d + 1) * cols] = right[d * rows : (d + 1) * rows, :]
        for r in range(lefts[0].shape[0] // rows):
            stacked = jnp.concatenate([left[r * rows : (r + 1) * rows, :] for left in lefts], axis=0)
            lall[r * LANES : (r + 1) * LANES, :] = stacked.T
        for d in range(extent):
            picked = map_ref[pl.ds(d, extent, stride=extent), :] * (1.0 / (parts * rows))
            maps[d * extent : (d + 1) * extent, :] = picked
        wt[...] = maps[...].T.astype(bf16)
        wide_t[...] = wide_ref[...].T
        shrink_t[...] = shrink_ref[...].T
        gains[...] = jnp.broadcast_to(down(gain_ref[...]), gains.shape)

    duo = 2
    size = block * extent
    first = pl.multiple_of(jnp.minimum(step, last - 1) * size, size)

    heights = 2 if block % 4 == 0 else 1
    height = block // heights

    def product(outer, n):
        c, v = n // heights, n % heights
        lanes = slice(c * duo * cols, (c + 1) * duo * cols)
        start = pl.multiple_of(first + v * height * extent, height * extent)
        made = dot(lall[pl.ds(start, height * extent), :], rall[:, lanes]).astype(bf16)
        for i in range(height):
            row = v * height + i
            for d in range(duo):
                at = (c * duo + d) * extent
                outer[row // 2, at : at + extent, row % 2 * cols : (row % 2 + 1) * cols] = made[
                    i * extent : (i + 1) * extent, d * cols : (d + 1) * cols
                ]

    def update(outer, k):
        mid = dot(wt[...], outer[k])
        middle[k] = mid + jnp.concatenate([pair_ref[2 * k].T, pair_ref[2 * k + 1].T], axis=1)

    def scale(k):
        normed[k] = (normalized_down(middle[k]) * gains[...]).astype(bf16)

    split = hidden.shape[1] // 2

    def widen(c, k):
        at = slice(c * split, (c + 1) * split)
        hidden[k, at, :] = jnp.maximum(dot(wide_t[at, :], normed[k]), 0.0).astype(bf16)

    def shrink(k):
        done = middle[k] + dot(shrink_t[...], hidden[k])
        for i in range(2):
            out_ref[2 * k + i] = done[:, i * cols : (i + 1) * cols].T

    pairs = block // 2

    def feed(outer):
        stages = (
            (0, functools.partial(update, outer)),
            (1, scale),
            (2, functools.partial(widen, 0)),
            (2, functools.partial(widen, 1)),
            (3, shrink),
        )
        pieces = []
        for t in range(pairs + 3):
            for lag, stage in stages:
                if 0 <= t - lag < pairs:
                    pieces.append(functools.partial(stage, t - lag))
        return pieces

    chunks = extent // duo * heights

    @pl.when(step == 0)
    def _():
        for c in range(chunks):
            product(outer_a, c)

    for odd, (made, used) in enumerate(((outer_a, outer_b), (outer_b, outer_a))):

        @pl.when((step > 0) & (step < last) & (step % 2 == odd))
        def _(made=made, used=used):
            pieces = feed(used)
            for n, piece in enumerate(pieces):
                for c in range(n * chunks // len(pieces), (n + 1) * chunks // len(pieces)):
                    product(made, c)
                piece()

        @pl.when((step == last) & (step % 2 == odd))
        def _(used=used):
            for piece in feed(used):
                piece()


def pair_update(lefts, rights, masks, upper, pair, maps, gain, wide, shrink, rows, block):
    parts = len(lefts)
    tile_rows, cols, channels = pair.shape
    extent = rights[0].shape[0] // rows
    pairs = block // 2
    whole = lambda shape: pl.BlockSpec(shape, lambda i: (0,) * len(shape))
    tile = pl.BlockSpec((block, cols, channels), lambda i: (jnp.maximum(i - 1, 0), 0, 0))
    return pl.pallas_call(
        functools.partial(pair_kernel, masks, upper, rows, extent),
        grid=(tile_rows // block + 1,),
        in_specs=[whole(a.shape) for a in (*lefts, *rights)]
        + [tile, whole(maps.shape), whole((1, channels)), whole(wide.shape), whole(shrink.shape)],
        out_specs=tile,
        out_shape=jax.ShapeDtypeStruct(pair.shape, jnp.float32),
        scratch_shapes=[
            pltpu.VMEM((parts * rows, extent * cols), jnp.bfloat16),
            pltpu.VMEM((tile_rows * extent, parts * rows), jnp.bfloat16),
            *[pltpu.VMEM((pairs, extent * extent, 2 * cols), jnp.bfloat16)] * 2,
            pltpu.VMEM((extent * extent, channels), jnp.float32),
            pltpu.VMEM((channels, extent * extent), jnp.bfloat16),
            pltpu.VMEM(wide.shape[::-1], jnp.bfloat16),
            pltpu.VMEM(shrink.shape[::-1], jnp.bfloat16),
            pltpu.VMEM((channels, 2 * cols), jnp.float32),
            pltpu.VMEM((pairs, channels, 2 * cols), jnp.float32),
            pltpu.VMEM((pairs, channels, 2 * cols), jnp.bfloat16),
            pltpu.VMEM((pairs, wide.shape[1], 2 * cols), jnp.bfloat16),
        ],
        name="pair_update",
        cost_estimate=pl.CostEstimate(
            flops=2 * tile_rows * cols * (extent * extent * (parts * rows + channels) + 2 * wide.size) * 2,
            bytes_accessed=pair.size * 8,
            transcendentals=tile_rows * cols,
        ),
    )(*lefts, *rights, pair, maps, gain.reshape(1, -1), wide, shrink)


def attention_kernel(
    heads, cols, x_ref, own_ref, far_ref, b0, b1, b2, b3, wq_ref, wk_ref, wv_ref, wo_ref, gain_ref, wide_ref,
    shrink_ref, out_ref, bias, natural, wq, wv, wo, wide_t, shrink_t, gains, masked, keys, values, score, weight,
    attended, middle, normed, hidden,
):
    step = pl.program_id(0)
    block, residues, features = x_ref.shape
    depth = features // heads
    half = residues // 2
    bf16 = jnp.bfloat16
    group = LANES // depth
    pairs = heads // 2
    units = block * pairs
    sides = features // LANES

    @pl.when(step == 0)
    def _():
        for h in range(heads):
            for r, tile in enumerate((b0, b1, b2, b3)):
                source = lax.axis_index("tile") ^ r
                top = pl.multiple_of(source // cols * half, half)
                edge = pl.multiple_of((source % cols ^ lax.axis_index("col")) * residues, residues)
                natural[pl.ds(top, half), pl.ds(edge, residues)] = tile[h].astype(jnp.float32) * LOG2E
            for side in range(2):
                bias[h // 2, side * residues : (side + 1) * residues, (h % 2) * residues : (h % 2 + 1) * residues] = (
                    natural[:, side * residues : (side + 1) * residues].T
                )
        for turned, ref in ((wq, wq_ref), (wv, wv_ref), (wo, wo_ref), (wide_t, wide_ref), (shrink_t, shrink_ref)):
            turned[...] = ref[...].T
        gains[...] = jnp.broadcast_to(down(gain_ref[...]), gains.shape)
        masked[...] = jnp.zeros_like(masked)
        for u in range(units):
            values[u, 2 * depth :, :] = jnp.ones((16, 2 * residues), bf16)

    def project():
        factor = LOG2E / (depth**0.5)
        own = own_ref[...].reshape(block * residues, features)
        far = far_ref[...].reshape(block * residues, features)
        query = (dot(wq[...], own, ((1,), (1,))) * factor).astype(bf16)
        for s in range(block):
            for h in range(heads):
                masked[
                    s * pairs + h // 2, h % group * depth : (h % group + 1) * depth, h % 2 * residues : (h % 2 + 1) * residues
                ] = query[h * depth : (h + 1) * depth, s * residues : (s + 1) * residues]
        for side, rows in enumerate((own, far)):
            key = dot(rows, wk_ref[...]).astype(bf16)
            value = dot(wv[...], rows, ((1,), (1,))).astype(bf16)
            for s in range(block):
                at = slice(s * residues, (s + 1) * residues)
                for f in range(sides):
                    keys[s, f, side * residues : (side + 1) * residues, :] = key[at, f * LANES : (f + 1) * LANES]
                for g in range(pairs):
                    values[s * pairs + g, : 2 * depth, side * residues : (side + 1) * residues] = value[
                        2 * g * depth : 2 * (g + 1) * depth, at
                    ]

    def stand():
        mid = x_ref[...].reshape(block * residues, features).T + dot(wo[...], attended[...])
        middle[...] = mid
        normed[...] = (normalized_down(mid) * gains[...]).astype(bf16)

    widths = 4
    chunk = hidden.shape[0] // widths
    part = features // 2

    def widen(c):
        at = slice(c * chunk, (c + 1) * chunk)
        hidden[at, :] = jnp.maximum(dot(wide_t[at, :], normed[...]), 0.0).astype(bf16)

    def shrink(c):
        at = slice(c * part, (c + 1) * part)
        done = middle[at, :] + dot(shrink_t[at, :], hidden[...])
        out_ref[:, :, at] = done.T.reshape(block, residues, part)

    feed = [functools.partial(widen, c) for c in range(widths)] + [functools.partial(shrink, c) for c in range(2)]

    def scores(u, i):
        s, g = u // pairs, u % pairs
        at = slice(i * residues, (i + 1) * residues)
        score[u % 2, at, :] = dot(keys[s, 2 * g // group, at, :], masked[u]) + bias[g, at, :]

    def soften(u, i):
        lanes = slice(i * residues, (i + 1) * residues)
        now = score[u % 2, :, lanes]
        weight[u % 2, :, lanes] = jnp.exp2(now - jnp.max(now, axis=0, keepdims=True)).astype(bf16)

    def attend(u):
        s, g = u // pairs, u % pairs
        out = dot(values[u], weight[u % 2])
        norm = 1.0 / out[2 * depth : 2 * depth + 1, :]
        for i in range(2):
            lanes = slice(i * residues, (i + 1) * residues)
            attended[(2 * g + i) * depth : (2 * g + i + 1) * depth, s * residues : (s + 1) * residues] = (
                out[i * depth : (i + 1) * depth, lanes] * norm[:, lanes]
            ).astype(bf16)

    def mix(left):
        for t in range(units + 2):
            for i in range(2):
                if i == 0 and t >= 2:
                    attend(t - 2)
                if t < units:
                    scores(t, i)
                turns, turn = 2 * (units + 2), 2 * t + i
                for piece in left[turn * len(left) // turns : (turn + 1) * len(left) // turns]:
                    piece()
                if 1 <= t <= units:
                    soften(t - 1, i)

    @pl.when(step == 0)
    def _():
        project()
        mix([])

    @pl.when((step > 0) & (step < pl.num_programs(0) - 1))
    def _():
        stand()
        project()
        mix(list(feed))

    @pl.when(step == pl.num_programs(0) - 1)
    def _():
        stand()
        for piece in feed:
            piece()


def attention(cols, x, own, far, biases, weights, gain, wide, shrink, block):
    rows, residues, features = x.shape
    heads = biases[0].shape[0]
    depth = features // heads
    units = block * heads // 2
    steps = rows // block
    wide_residues = 2 * residues
    whole = lambda shape: pl.BlockSpec(shape, lambda i: (0,) * len(shape))
    tile = pl.BlockSpec((block, residues, features), lambda i: (jnp.minimum(i, steps - 1), 0, 0))
    late = pl.BlockSpec((block, residues, features), lambda i: (jnp.maximum(i - 1, 0), 0, 0))
    return pl.pallas_call(
        functools.partial(attention_kernel, heads, cols),
        grid=(steps + 1,),
        in_specs=[late, tile, tile]
        + [whole(b.shape) for b in biases]
        + [whole(w.shape) for w in weights]
        + [whole((1, features)), whole(wide.shape), whole(shrink.shape)],
        out_specs=late,
        scratch_shapes=[
            pltpu.VMEM((heads // 2, wide_residues, wide_residues), jnp.float32),
            pltpu.VMEM((residues, wide_residues), jnp.float32),
            *[pltpu.VMEM((features, features), jnp.bfloat16)] * 3,
            pltpu.VMEM(wide.shape[::-1], jnp.bfloat16),
            pltpu.VMEM(shrink.shape[::-1], jnp.bfloat16),
            pltpu.VMEM((features, block * residues), jnp.float32),
            pltpu.VMEM((units, LANES, wide_residues), jnp.bfloat16),
            pltpu.VMEM((block, features // LANES, wide_residues, LANES), jnp.bfloat16),
            pltpu.VMEM((units, 2 * depth + 16, wide_residues), jnp.bfloat16),
            pltpu.VMEM((2, wide_residues, wide_residues), jnp.float32),
            pltpu.VMEM((2, wide_residues, wide_residues), jnp.bfloat16),
            pltpu.VMEM((features, block * residues), jnp.bfloat16),
            pltpu.VMEM((features, block * residues), jnp.float32),
            pltpu.VMEM((features, block * residues), jnp.bfloat16),
            pltpu.VMEM((wide.shape[1], block * residues), jnp.bfloat16),
        ],
        out_shape=jax.ShapeDtypeStruct(x.shape, jnp.float32),
        name="attention",
        cost_estimate=pl.CostEstimate(
            flops=2 * rows * residues * (6 * features * features + 4 * heads * residues * features + 2 * wide.size),
            bytes_accessed=rows * residues * features * 12,
            transcendentals=rows * residues * heads * 2 * residues,
        ),
    )(x, own, far, *biases, *weights, gain.reshape(1, -1), wide, shrink)


def exchanged(
    alignment_tensor,
    residue_grid,
    mixing_scale_vector,
    logit_offset_scale,
    feedforward_scale,
    product_scale_vector,
    grid_scale_vector,
    logit_offset_map,
    asking_mapping,
    lookup_mapping,
    content_mapping,
    mixing_return_matrix,
    alignment_widen_map,
    alignment_shrink_map,
    former_embedding_map,
    latter_embedding_map,
    product_return_map,
    grid_widen_map,
    grid_shrink_map,
):
    msa, pair = alignment_tensor[0], residue_grid[0]
    rows = msa.shape[0]
    tiles = lax.axis_size("tile")
    upper = tiles // 2

    def swap(value, axis, mask):
        return lax.ppermute(value, axis, [(i, i ^ mask) for i in range(lax.axis_size(axis))])

    cols = lax.axis_size("col")
    normed, even, odd, right = factors(
        msa,
        mixing_scale_vector,
        product_scale_vector,
        former_embedding_map.T,
        latter_embedding_map.T,
        upper,
        min(rows, 8),
    )
    devices = [(t, c) for t in range(tiles) for c in range(cols)]

    def route(value, goal):
        pairs = [(t * cols + c, goal(t, c)[0] * cols + goal(t, c)[1]) for t, c in devices]
        return lax.ppermute(value, ("tile", "col"), pairs)

    def owner(r):
        def goal(t, c):
            aim = t ^ r
            return (aim, c) if aim // upper == c else (aim ^ upper, 1 - c)

        return goal

    right_up = swap(right, "tile", upper)
    lefts = []
    for r in range(tiles):
        lefts.append(route(odd if r % upper else even, owner(r)))
    right_side = swap(right, "tile", 1)
    normed_far = swap(normed, "col", 1)

    pair, _ = lax.optimization_barrier((pair, right))
    tile_bias = pair_bias(pair, logit_offset_scale, logit_offset_map.T, min(pair.shape[0], 32))
    tile_bias, right_up = lax.optimization_barrier((tile_bias, right_up))
    rights = [right, right_up, right_side, swap(right_up, "tile", 1)]
    masks = (0, upper, 1, upper + 1)
    biases = [
        route(tile_bias, lambda t, c, r=r: ((t % upper * cols + c) ^ r, t // upper)) for r in range(tiles)
    ]

    grid_revised = pair_update(
        lefts, rights, masks, upper, pair, product_return_map, grid_scale_vector, grid_widen_map, grid_shrink_map, rows, 16
    )
    alignment_revised = attention(
        cols,
        msa,
        normed,
        normed_far,
        biases,
        (asking_mapping, lookup_mapping, content_mapping, mixing_return_matrix),
        feedforward_scale,
        alignment_widen_map,
        alignment_shrink_map,
        4,
    )
    return (alignment_revised[None], grid_revised[None])


def on_device(*args):
    msa, pair = args[0], args[1]
    extent = args[14].shape[1]
    fits = (
        lax.axis_size("col") == 2
        and lax.axis_size("tile") == 4
        and msa.shape[1] % 16 == 0
        and msa.shape[2] == LANES
        and pair.shape[1] % 16 == 0
        and pair.shape[2] == LANES
        and LANES % extent == 0
        and extent % 16 == 0
    )
    if not fits:
        return gathered(*args)
    return exchanged(*args)


def solution(mesh):
    placed = (
        P(("groups", "branch"), "tile", "col", None),
        P(("groups", "branch"), "tile", "col", None),
        P(),
        P(),
        P(),
        P(),
        P(),
        P(),
        P(),
        P(),
        P(),
        P(),
        P(),
        P(),
        P(),
        P(),
        P(),
        P(),
        P(),
    )
    return jax.shard_map(
        on_device,
        mesh=mesh,
        in_specs=placed,
        out_specs=(
            P(("groups", "branch"), "tile", "col", None),
            P(("groups", "branch"), "tile", "col", None),
        ),
        check_vma=False,
    )
```
